512 devices in a mesh: tile: 64 (over z, y_lo, core), inner: 8 (over x, y_hi).
Axes of the slice: x: 4, y: 4 (y_hi: 2, y_lo: 2; y = y_hi * 2 + y_lo), z: 16, core: 2. Of those that a mesh axis runs over, the one named last changes fastest.
Arguments:
- amplitudes: bfloat16 [512, 16384], P('tile', 'inner'), may hold values from -6 to 6
- left_factors: bfloat16 [1024, 16384], P('tile', 'inner'), may hold values from -0.1875 to 0.1875
- right_factors: bfloat16 [1024, 65536], P(None, 'tile'), may hold values from -0.1875 to 0.1875
- tile_pattern: int32 [32, 128], replicated, may hold values from 0 to 1, as said below
- occupied_shift: float32 [512], P('inner'), may hold values from 0.5 to 2
- virtual_shift: float32 [65536], P('tile'), may hold values from 0.5 to 5
Outputs:
- residual: float32 [512, 65536], P('inner', 'tile')
The draws below stay inside these ranges and needn't reach their ends.
Inputs may be any that keep to these rules, and one draw needn't show every extreme that they name: `tile_pattern`: 1 where the tiles interact, 0 where their integrals are dropped.
All inputs are finite; a program needn't handle non-finite values.
Results may differ from the reference program's by a relative error of at most 0.0029.
Values may be sent and summed in bfloat16 or wider, within the bound.
A program may use at most 64 MiB of HBM per device.

```python
import math
import jax
import jax.numpy as jnp
from jax import lax

NAUX = 1024
TILE = 512
ROWS = 512
QP = 16384
PP = 65536


def draw_tile_pattern(key, part):
    level_key, cell_key = jax.random.split(jax.random.fold_in(key, 7))
    levels = jax.random.randint(level_key, (1, PP // TILE), 0, 4)
    limits = jnp.array([3, 6, 9, 16], jnp.int32)[levels]
    cells = jax.random.randint(cell_key, (QP // TILE, PP // TILE), 0, 24)
    return (cells < limits).astype(jnp.int32)


def block_levels(key, extent, shards, smallest, largest):
    level, own = 1.0, jax.random.fold_in(key, 6)
    for position, shards_of in shards:
        steps = jnp.exp(jax.random.uniform(jax.random.fold_in(own, position), (shards_of,), jnp.float32, smallest / len(shards), largest / len(shards)))
        level = level * jnp.repeat(steps, extent[position] // shards_of).reshape([-1 if axis == position else 1 for axis in range(len(extent))])
    return level


def normal_values(key, dims, spread, reach, pieces=(), kind=jnp.bfloat16):
    result = spread * jax.random.normal(key, dims, jnp.float32)
    if pieces:
        result = result * block_levels(key, dims, pieces, -0.22, 0.18)
    return jnp.clip(result, -reach, reach).astype(kind)


def setup_inputs(seed: int = 0) -> dict:
    arg_keys = jax.random.split(jax.random.key(seed), 7)
    amplitudes = normal_values(arg_keys[0], (ROWS, QP), 1.0, 6.0, ((0, 64), (1, 8)))
    left_factors = normal_values(arg_keys[1], (NAUX, QP), NAUX ** -0.5, 0.1875, ((0, 64), (1, 8)))
    right_factors = normal_values(arg_keys[2], (NAUX, PP), NAUX ** -0.5, 0.1875, ((1, 64),))
    tile_pattern = draw_tile_pattern(jax.random.fold_in(arg_keys[6], 71), 0)
    occupied_shift = jnp.clip(jnp.exp(math.log(2.0) - 1.3862944 * jax.random.uniform(arg_keys[4], (ROWS,), jnp.float32) ** block_levels(arg_keys[4], (ROWS,), ((0, 8),), -0.2, 0.2)), 0.5, 2.0)
    virtual_shift = jnp.clip(jnp.exp(math.log(5.0) - 2.3025851 * jax.random.uniform(arg_keys[5], (PP,), jnp.float32) ** block_levels(arg_keys[5], (PP,), ((0, 64),), -0.2, 0.2)), 0.5, 5.0)
    return dict(amplitudes=amplitudes, left_factors=left_factors, right_factors=right_factors, tile_pattern=tile_pattern, occupied_shift=occupied_shift, virtual_shift=virtual_shift)


def reference(amplitudes, left_factors, right_factors, tile_pattern, occupied_shift, virtual_shift):
    left_tiles = QP // TILE
    right_tiles = PP // TILE

    def column(right_index):
        right_index = right_index.astype(jnp.int32)
        right_cols = lax.dynamic_slice_in_dim(right_factors, right_index * TILE, TILE, 1)

        def visit_tile(left_index, totals):
            left_index = jnp.asarray(left_index).astype(jnp.int32)

            def include(current):
                left_cols = lax.dynamic_slice_in_dim(left_factors, left_index * TILE, TILE, 1)
                integral = lax.dot_general(left_cols, right_cols, (((0,), (0,)), ((), ())), preferred_element_type=jnp.float32).astype(jnp.bfloat16)
                amplitude_tile = lax.dynamic_slice_in_dim(amplitudes, left_index * TILE, TILE, 1)
                return current + jnp.dot(amplitude_tile, integral, preferred_element_type=jnp.float32)

            return lax.cond(tile_pattern[left_index, right_index] != 0, include, lambda current: current, totals)

        return lax.fori_loop(0, left_tiles, visit_tile, jnp.zeros((ROWS, TILE), jnp.float32))

    blocks = lax.map(column, jnp.arange(right_tiles, dtype=jnp.int32))
    ladder = jnp.transpose(blocks, (1, 0, 2)).reshape(ROWS, PP)
    return ladder / (occupied_shift[:, None] + virtual_shift[None, :])
```

```python
import functools

import jax
import jax.numpy as jnp
from jax import lax
from jax.experimental import pallas as pl
from jax.experimental.pallas import tpu as pltpu
from jax.sharding import Mesh
from jax.sharding import PartitionSpec as P

TILE = 512
TILE_AXES = ("z", "y", "core")
MESH_ID = pl.DeviceIdType.MESH
PLANES = 16
INNER = 8
QUADS = 4
HALVES = 2
LEFT = 4
RIGHT = 128
ROWS = 8
DEPTH = 64
LANES = 128
GROUP = PLANES * QUADS


def kernel(
    a_ref, l_ref, r_ref, pattern_ref, out_ref,
    a_all, l_all, r_all, kron, m_out, m_in, s_out, s_in,
    ring_send, ring_recv, near_send, near_recv, m_send, m_recv, s_send, s_recv, own_sem,
):
    z = lax.axis_index("z")
    y = lax.axis_index("y")
    core = lax.axis_index("core")
    inner = lax.axis_index("inner")
    quad = y * 2 + core
    place = z * QUADS + quad
    pair = (z // 2) * 2
    parity = z % 2

    def tile_device(spot):
        return dict(z=spot // QUADS, y=(spot // 2) % 2, core=spot % 2, inner=inner)

    def mix_device(spot):
        return dict(z=pair + spot % 2, y=y, core=core, inner=spot // 2)

    mix_place = inner * 2 + parity
    barrier = pltpu.get_barrier_semaphore()

    @pl.loop(1, GROUP)
    def _(step):
        pl.semaphore_signal(
            barrier, 1, device_id=tile_device((place + step) % GROUP), device_id_type=MESH_ID
        )

    @pl.loop(0, INNER)
    def _(other):
        @pl.when(other != inner)
        def _():
            for side in range(2):
                pl.semaphore_signal(
                    barrier, 1, device_id=mix_device(other * 2 + side), device_id_type=MESH_ID
                )

    own_a = pltpu.make_async_copy(a_ref, a_all.at[z], own_sem.at[0])
    own_l = pltpu.make_async_copy(l_ref, l_all.at[quad], own_sem.at[1])
    own_r = pltpu.make_async_copy(r_ref, r_all, own_sem.at[2])
    own_a.start()
    own_l.start()
    own_r.start()
    pl.semaphore_wait(barrier, GROUP - 1 + 2 * (INNER - 1))

    span = a_ref.shape[1] // HALVES

    def hop(way, step, half):
        toward = 1 if way == 0 else PLANES - 1
        back = PLANES - step if way == 0 else step
        origin = (z + back) % PLANES
        columns = pl.ds(half * span, span)
        src = a_ref.at[:, columns] if step == 0 else a_all.at[origin, :, columns]
        return pltpu.make_async_remote_copy(
            src_ref=src,
            dst_ref=a_all.at[origin, :, columns],
            send_sem=ring_send.at[way, step, half],
            recv_sem=ring_recv.at[way, step, half],
            device_id=dict(z=(z + toward) % PLANES, y=y, core=core, inner=inner),
            device_id_type=MESH_ID,
        )

    def hops(step):
        if step < PLANES // 2 - 1:
            return [hop(way, step, half) for half in range(HALVES) for way in range(2)]
        return [hop(half, step, half) for half in range(HALVES)]

    ring = [hops(step) for step in range(PLANES // 2)]
    for copy in ring[0]:
        copy.start()

    def near_copy(step):
        other = (quad + step) % QUADS
        return pltpu.make_async_remote_copy(
            src_ref=l_ref,
            dst_ref=l_all.at[quad],
            send_sem=near_send.at[step - 1],
            recv_sem=near_recv.at[step - 1],
            device_id=dict(z=z, y=other // 2, core=other % 2, inner=inner),
            device_id_type=MESH_ID,
        )

    near = [near_copy(step) for step in range(1, QUADS)]
    for copy in near:
        copy.start()

    mask = jnp.where(pattern_ref[...] != 0, 1.0, 0.0).astype(jnp.bfloat16)
    spread = jnp.where(
        lax.broadcasted_iota(jnp.int32, (32, 256), 0)
        == lax.broadcasted_iota(jnp.int32, (32, 256), 1) >> 3,
        1.0,
        0.0,
    ).astype(jnp.bfloat16)
    spread = lax.dot_general(
        mask, spread, (((0,), (0,)), ((), ())), preferred_element_type=jnp.float32
    ).astype(jnp.bfloat16)
    same = jnp.where(
        (lax.broadcasted_iota(jnp.int32, (LANES, 256), 0) & 7)
        == (lax.broadcasted_iota(jnp.int32, (LANES, 256), 1) & 7),
        1.0,
        0.0,
    )
    lifted = lax.broadcasted_iota(jnp.int32, (LANES, RIGHT), 1) - (
        lax.broadcasted_iota(jnp.int32, (LANES, RIGHT), 0) >> 3
    )

    @pl.loop(0, RIGHT // 16)
    def _(block):
        lift = jnp.where(lifted == block * 16, 1.0, 0.0).astype(jnp.bfloat16)
        rows = jnp.dot(lift, spread, preferred_element_type=jnp.float32)
        kron[pl.ds(pl.multiple_of(block * LANES, LANES), LANES), :] = (rows * same).astype(
            jnp.bfloat16
        )

    for step in range(PLANES // 2 - 1):
        for now, later in zip(ring[step], ring[step + 1] if step < PLANES // 2 - 2 else [None] * 4):
            now.wait_recv()
            if later is not None:
                later.start()
        if step == PLANES // 2 - 2:
            for later in ring[step + 1]:
                later.start()
    for copy in ring[-1]:
        copy.wait_recv()
    own_a.wait()
    own_l.wait()
    for copy in near:
        copy.wait_recv()

    left_side = lax.broadcasted_iota(jnp.int32, (PLANES * ROWS, LANES), 1) < DEPTH
    for couple in range(LEFT // 2):
        wide = []
        for left in (couple * 2, couple * 2 + 1):
            columns = pl.ds(left * TILE, TILE)
            factors = l_all[:, :, columns].reshape(DEPTH, TILE)
            wide.append(
                lax.dot_general(
                    a_all[:, :, columns].reshape(PLANES * ROWS, TILE),
                    jnp.concatenate([factors, factors], axis=0),
                    (((1,), (1,)), ((), ())),
                    preferred_element_type=jnp.float32,
                )
            )
        m_out[:, couple] = jnp.where(left_side, *wide).reshape(PLANES, ROWS, LANES)

    def mix_copy(spot):
        return pltpu.make_async_remote_copy(
            src_ref=m_out.at[spot],
            dst_ref=m_in.at[mix_place],
            send_sem=m_send.at[spot],
            recv_sem=m_recv.at[mix_place],
            device_id=mix_device(spot),
            device_id_type=MESH_ID,
        )

    @pl.loop(1, 2 * INNER)
    def _(step):
        mix_copy((mix_place + step) % (2 * INNER)).start()

    m_in[mix_place] = m_out[mix_place]

    def mix_arrival(spot):
        return pltpu.make_async_remote_copy(
            src_ref=m_out.at[spot],
            dst_ref=m_in.at[spot],
            send_sem=m_send.at[spot],
            recv_sem=m_recv.at[spot],
            device_id=mix_device(spot),
            device_id_type=MESH_ID,
        )

    @pl.loop(1, 2 * INNER)
    def _(step):
        mix_arrival((mix_place + 2 * INNER - step) % (2 * INNER)).wait_recv()

    tall = m_in[...].reshape(INNER, 2, LEFT // 2, ROWS, LANES)
    even = tall[:, 0].reshape(INNER * LEFT // 2 * ROWS, LANES)
    odd = tall[:, 1].reshape(INNER * LEFT // 2 * ROWS, LANES)
    first = jnp.where(left_side, even, pltpu.roll(odd, DEPTH, 1))
    second = jnp.where(left_side, pltpu.roll(even, DEPTH, 1), odd)
    stacked = jnp.concatenate(
        [
            first.reshape(INNER * LEFT // 2, 1, ROWS, LANES),
            second.reshape(INNER * LEFT // 2, 1, ROWS, LANES),
        ],
        axis=1,
    ).reshape(INNER * LEFT * ROWS, LANES)
    high = stacked.astype(jnp.bfloat16)
    low = (stacked - high.astype(jnp.float32)).astype(jnp.bfloat16)
    split = jnp.concatenate([high, low], axis=1)

    def tile_copy(spot):
        return pltpu.make_async_remote_copy(
            src_ref=s_out.at[spot],
            dst_ref=s_in.at[place],
            send_sem=s_send.at[spot],
            recv_sem=s_recv.at[place],
            device_id=tile_device(spot),
            device_id_type=MESH_ID,
        )

    def tile_arrival(spot):
        return pltpu.make_async_remote_copy(
            src_ref=s_out.at[spot],
            dst_ref=s_in.at[spot],
            send_sem=s_send.at[spot],
            recv_sem=s_recv.at[spot],
            device_id=tile_device(spot),
            device_id_type=MESH_ID,
        )

    chunks = 4
    per = GROUP // chunks
    lead = (z // (PLANES // chunks)) * per
    for chunk in range(chunks):
        base = pl.multiple_of((lead + (chunk + 2) % chunks * per) % GROUP, per)
        rows = pl.ds(pl.multiple_of(base * 2 * ROWS, LANES), per * 2 * ROWS)
        both = jnp.dot(kron[rows, :], split, preferred_element_type=jnp.float32)
        s_out[pl.ds(base, per)] = (
            (both[:, :LANES] + both[:, LANES:]).astype(jnp.bfloat16).reshape(per, 2 * ROWS, LANES)
        )

        @pl.loop(0, per)
        def _(step):
            spot = base + (step + place) % per

            @pl.when(spot != place)
            def _():
                tile_copy(spot).start()

    s_in[place] = s_out[place]
    own_r.wait()

    @pl.loop(1, GROUP)
    def _(step):
        tile_arrival((place + step) % GROUP).wait_recv()

    mixed = jnp.concatenate(
        [s_in[pl.ds(eight * 8, 8)].reshape(LANES, LANES) for eight in range(GROUP // 8)], axis=1
    )
    for side in range(2):
        columns = pl.ds(side * TILE, TILE)
        ladder = jnp.dot(mixed, r_all[:, columns], preferred_element_type=jnp.float32)
        ladder = ladder.reshape(8, 2, ROWS, TILE)[:, side]
        out_ref[:, columns] = ladder.reshape(8 * ROWS, TILE)

    for copies in ring:
        for copy in copies:
            copy.wait_send()
    for copy in near:
        copy.wait_send()

    @pl.loop(1, 2 * INNER)
    def _(step):
        mix_arrival((mix_place + step) % (2 * INNER)).wait_send()

    @pl.loop(1, GROUP)
    def _(step):
        tile_arrival((place + step) % GROUP).wait_send()


def on_device(amplitudes, left_factors, right_factors, tile_pattern, occupied_shift, virtual_shift):
    width = amplitudes.shape[1]
    out_width = right_factors.shape[1]
    ladder = pl.pallas_call(
        kernel,
        name="ladder",
        out_shape=jax.ShapeDtypeStruct((occupied_shift.shape[0], out_width), jnp.float32),
        in_specs=[pl.BlockSpec(memory_space=pl.ANY)] * 3
        + [pl.BlockSpec(memory_space=pltpu.VMEM)],
        out_specs=pl.BlockSpec(memory_space=pltpu.VMEM),
        scratch_shapes=[
            pltpu.VMEM((PLANES, ROWS, width), jnp.bfloat16),
            pltpu.VMEM((QUADS, DEPTH // QUADS, width), jnp.bfloat16),
            pltpu.VMEM(right_factors.shape, jnp.bfloat16),
            pltpu.VMEM((RIGHT * ROWS, 2 * LANES), jnp.bfloat16),
            pltpu.VMEM((2 * INNER, LEFT // 2, ROWS, LANES), jnp.float32),
            pltpu.VMEM((2 * INNER, LEFT // 2, ROWS, LANES), jnp.float32),
            pltpu.VMEM((GROUP, 2 * ROWS, LANES), jnp.bfloat16),
            pltpu.VMEM((GROUP, 2 * ROWS, LANES), jnp.bfloat16),
            pltpu.SemaphoreType.DMA((2, PLANES // 2, HALVES)),
            pltpu.SemaphoreType.DMA((2, PLANES // 2, HALVES)),
            pltpu.SemaphoreType.DMA((QUADS - 1,)),
            pltpu.SemaphoreType.DMA((QUADS - 1,)),
            pltpu.SemaphoreType.DMA((2 * INNER,)),
            pltpu.SemaphoreType.DMA((2 * INNER,)),
            pltpu.SemaphoreType.DMA((GROUP,)),
            pltpu.SemaphoreType.DMA((GROUP,)),
            pltpu.SemaphoreType.DMA((3,)),
        ],
        compiler_params=pltpu.CompilerParams(
            collective_id=0, has_side_effects=True, vmem_limit_bytes=32 << 20
        ),
    )(amplitudes, left_factors, right_factors, tile_pattern)
    return ladder / (occupied_shift[:, None] + virtual_shift[None, :])


def solution(mesh):
    torus = Mesh(
        mesh.devices.reshape(PLANES, 2, 2, mesh.shape["inner"]), (*TILE_AXES, "inner")
    )
    placed = (
        P(TILE_AXES, "inner"),
        P(TILE_AXES, "inner"),
        P(None, TILE_AXES),
        P(),
        P("inner"),
        P(TILE_AXES),
    )
    return jax.shard_map(
        on_device, mesh=torus, in_specs=placed, out_specs=P("inner", TILE_AXES), check_vma=False
    )
```

```python
import jax
import jax.numpy as jnp
from jax import lax
from jax.experimental import pallas as pl
from jax.experimental.pallas import tpu as pltpu
from jax.sharding import Mesh
from jax.sharding import PartitionSpec as P

TILE = 512
TILE_AXES = ("z", "y", "core")
MESH_ID = pl.DeviceIdType.MESH
PLANES = 16
PAIRS = 8
INNER = 8
QUADS = 4
LEFT = 4
RIGHT = 128
ROWS = 8
DEPTH = 16
LANES = 128
GROUP = PLANES * QUADS
CHUNKS = 4
PER = GROUP // CHUNKS
LAG = 8
ORDER = (1, 7, 2, 6, 3, 5, 4)


def turn(step):
    return jnp.where(step % 2 == 1, (step + 1) // 2, (PAIRS - step // 2) % PAIRS)


def kernel(
    a_ref, l_ref, r_ref, pattern_ref, out_ref,
    a_all, l_all, r_all, pattern, kron, m_out, m_in, s_out, s_in,
    gather_send, gather_recv, near_send, near_recv, m_send, m_recv, s_send, s_recv, own_sem, ready,
):
    z = lax.axis_index("z")
    y = lax.axis_index("y")
    core = lax.axis_index("core")
    inner = lax.axis_index("inner")
    quad = y * 2 + core
    place = z * QUADS + quad
    pair = z // 2
    parity = z % 2

    def plane_device(plane):
        return dict(z=plane, y=y, core=core, inner=inner)

    def near_device(step):
        return dict(
            z=z,
            y=y if step == 1 else 1 - y,
            core=core if step == 2 else 1 - core,
            inner=inner,
        )

    def near_quad(step):
        return (y if step == 1 else 1 - y) * 2 + (core if step == 2 else 1 - core)

    def inner_device(other):
        return dict(z=z, y=y, core=core, inner=other)

    def tile_device(spot):
        return dict(z=spot >> 2, y=(spot >> 1) & 1, core=spot & 1, inner=inner)

    def greet(semaphore, device):
        pl.semaphore_signal(semaphore, 1, device_id=device, device_id_type=MESH_ID)

    barrier = pltpu.get_barrier_semaphore()
    for step in range(1, PLANES):
        greet(barrier, plane_device((z + step) % PLANES))
    for step in (1, 2, 3):
        greet(barrier, near_device(step))
    for step in range(1, INNER):
        greet(barrier, inner_device((inner + step) % INNER))

    own_a = pltpu.make_async_copy(a_ref, a_all.at[pair], own_sem.at[0])
    own_l = pltpu.make_async_copy(l_ref, l_all.at[parity, quad], own_sem.at[1])
    own_r = pltpu.make_async_copy(r_ref, r_all, own_sem.at[2])
    own_p = pltpu.make_async_copy(pattern_ref, pattern, own_sem.at[3])
    own_a.start()
    own_l.start()
    own_p.start()
    own_r.start()
    pl.semaphore_wait(barrier, PLANES - 1 + QUADS - 1 + INNER - 1)

    def factor_copy(src, side, step):
        spot = side * 4 + step
        mine = parity if side == 0 else 1 - parity
        return pltpu.make_async_remote_copy(
            src_ref=src,
            dst_ref=l_all.at[mine, quad],
            send_sem=near_send.at[spot],
            recv_sem=near_recv.at[spot],
            device_id=near_device(step) if step else plane_device(pair * 2 + 1 - parity),
            device_id_type=MESH_ID,
        )

    def factor_arrival(side, step):
        spot = side * 4 + step
        mine = parity if side == 0 else 1 - parity
        if step == 0:
            dst = l_all.at[1 - parity, quad]
        else:
            dst = l_all.at[mine, near_quad(step)]
        return pltpu.make_async_remote_copy(
            src_ref=l_ref,
            dst_ref=dst,
            send_sem=near_send.at[spot],
            recv_sem=near_recv.at[spot],
            device_id=plane_device(z),
            device_id_type=MESH_ID,
        )

    def gather_copy(step):
        return pltpu.make_async_remote_copy(
            src_ref=a_ref,
            dst_ref=a_all.at[pair],
            send_sem=gather_send.at[step],
            recv_sem=gather_recv.at[pair],
            device_id=plane_device((pair + step) % PAIRS * 2 + parity),
            device_id_type=MESH_ID,
        )

    def gather_arrival(source):
        return pltpu.make_async_remote_copy(
            src_ref=a_ref,
            dst_ref=a_all.at[source],
            send_sem=gather_send.at[0],
            recv_sem=gather_recv.at[source],
            device_id=plane_device(z),
            device_id_type=MESH_ID,
        )

    shared = [factor_copy(l_ref, 0, step) for step in range(4)]
    gathered = [gather_copy(step) for step in ORDER]
    for copy in shared + gathered:
        copy.start()
    for step in (1, 2, 3):
        greet(ready, near_device(step))

    own_p.wait()
    mask = jnp.where(pattern[...] != 0, 1.0, 0.0).astype(jnp.bfloat16)
    spread = jnp.where(
        lax.broadcasted_iota(jnp.int32, (32, 256), 0)
        == lax.broadcasted_iota(jnp.int32, (32, 256), 1) >> 3,
        1.0,
        0.0,
    ).astype(jnp.bfloat16)
    spread = lax.dot_general(
        mask, spread, (((0,), (0,)), ((), ())), preferred_element_type=jnp.float32
    ).astype(jnp.bfloat16)
    same = jnp.where(
        (lax.broadcasted_iota(jnp.int32, (LANES, 256), 0) & 7)
        == (lax.broadcasted_iota(jnp.int32, (LANES, 256), 1) & 7),
        1.0,
        0.0,
    )
    lifted = lax.broadcasted_iota(jnp.int32, (LANES, RIGHT), 1) - (
        lax.broadcasted_iota(jnp.int32, (LANES, RIGHT), 0) >> 3
    )

    @pl.loop(0, RIGHT // 16)
    def _(block):
        lift = jnp.where(lifted == block * 16, 1.0, 0.0).astype(jnp.bfloat16)
        rows = jnp.dot(lift, spread, preferred_element_type=jnp.float32)
        kron[pl.ds(pl.multiple_of(block * LANES, LANES), LANES), :] = (rows * same).astype(
            jnp.bfloat16
        )

    factor_arrival(0, 0).wait_recv()
    passed = [factor_copy(l_all.at[1 - parity, quad], 1, step) for step in (1, 2, 3)]
    for copy in passed:
        copy.start()
    own_a.wait()
    own_l.wait()
    for side in range(2):
        for step in (1, 2, 3):
            factor_arrival(side, step).wait_recv()

    def mix_copy(other):
        return pltpu.make_async_remote_copy(
            src_ref=m_out.at[other],
            dst_ref=m_in.at[inner],
            send_sem=m_send.at[other],
            recv_sem=m_recv.at[inner],
            device_id=inner_device(other),
            device_id_type=MESH_ID,
        )

    def mix_arrival(other):
        return pltpu.make_async_remote_copy(
            src_ref=m_out.at[other],
            dst_ref=m_in.at[other],
            send_sem=m_send.at[other],
            recv_sem=m_recv.at[other],
            device_id=inner_device(other),
            device_id_type=MESH_ID,
        )

    def tile_copy(spot):
        return pltpu.make_async_remote_copy(
            src_ref=s_out.at[spot],
            dst_ref=s_in.at[place],
            send_sem=s_send.at[spot],
            recv_sem=s_recv.at[place],
            device_id=tile_device(spot),
            device_id_type=MESH_ID,
        )

    def tile_arrival(spot):
        return pltpu.make_async_remote_copy(
            src_ref=s_out.at[spot],
            dst_ref=s_in.at[spot],
            send_sem=s_send.at[spot],
            recv_sem=s_recv.at[spot],
            device_id=tile_device(spot),
            device_id_type=MESH_ID,
        )

    lead = (z >> 2) * PER

    @pl.loop(0, PAIRS + LAG)
    def _(step):
        @pl.when(step < PAIRS)
        def _():
            other = (pair + turn(step)) % PAIRS

            @pl.when(step > 0)
            def _():
                gather_arrival(other).wait_recv()

            for left in range(LEFT):
                columns = pl.ds(left * TILE, TILE)
                m_out[other, left] = lax.dot_general(
                    a_all[other, :, columns],
                    l_all[:, :, :, columns].reshape(LANES, TILE),
                    (((1,), (1,)), ((), ())),
                    preferred_element_type=jnp.float32,
                )

            @pl.when(other != inner)
            def _():
                mix_copy(other).start()

            @pl.when(other == inner)
            def _():
                m_in[inner] = m_out[inner]

        @pl.when((step >= LAG) & ((pair + turn(step - LAG)) % PAIRS == inner))
        def _():
            pl.semaphore_wait(ready, QUADS - 1)

            @pl.loop(1, INNER)
            def _(more):
                mix_arrival((inner + more) % INNER).wait_recv()

            stacked = m_in[...].reshape(INNER * LEFT * ROWS, LANES)
            high = stacked.astype(jnp.bfloat16)
            low = (stacked - high.astype(jnp.float32)).astype(jnp.bfloat16)
            split = jnp.concatenate([high, low], axis=1)
            for chunk in range(CHUNKS):
                base = pl.multiple_of((lead + (chunk + 2) % CHUNKS * PER) % GROUP, PER)
                rows = pl.ds(pl.multiple_of(base * 2 * ROWS, LANES), PER * 2 * ROWS)
                both = jnp.dot(kron[rows, :], split, preferred_element_type=jnp.float32)
                both = both[:, :LANES] + both[:, LANES:]
                s_out[pl.ds(base, PER)] = both.astype(jnp.bfloat16).reshape(PER, 2 * ROWS, LANES)

                @pl.loop(0, PER)
                def _(more):
                    spot = base + ((more + place) & (PER - 1))

                    @pl.when(spot != place)
                    def _():
                        tile_copy(spot).start()

            s_in[place] = s_out[place]

    own_r.wait()

    @pl.loop(1, GROUP)
    def _(step):
        tile_arrival((place + step) & (GROUP - 1)).wait_recv()

    mixed = jnp.concatenate(
        [s_in[pl.ds(eight * 8, 8)].reshape(LANES, LANES) for eight in range(GROUP // 8)], axis=1
    )
    for side in range(2):
        columns = pl.ds(side * TILE, TILE)
        ladder = jnp.dot(mixed, r_all[:, columns], preferred_element_type=jnp.float32)
        ladder = ladder.reshape(8, 2, ROWS, TILE)[:, side]
        out_ref[:, columns] = ladder.reshape(8 * ROWS, TILE)

    for copy in shared + passed + gathered:
        copy.wait_send()

    @pl.loop(1, INNER)
    def _(step):
        mix_arrival((inner + step) % INNER).wait_send()

    @pl.loop(1, GROUP)
    def _(step):
        tile_arrival((place + step) & (GROUP - 1)).wait_send()


def on_device(amplitudes, left_factors, right_factors, tile_pattern, occupied_shift, virtual_shift):
    width = amplitudes.shape[1]
    out_width = right_factors.shape[1]
    operands = (amplitudes, left_factors, right_factors, tile_pattern)
    ladder = pl.pallas_call(
        kernel,
        name="ladder",
        out_shape=jax.ShapeDtypeStruct((occupied_shift.shape[0], out_width), jnp.float32),
        in_specs=[pl.BlockSpec(memory_space=pltpu.HBM)] * 4,
        out_specs=pl.BlockSpec(memory_space=pltpu.VMEM),
        scratch_shapes=[
            pltpu.VMEM((PAIRS, ROWS, width), jnp.bfloat16),
            pltpu.VMEM((2, QUADS, DEPTH, width), jnp.bfloat16),
            pltpu.VMEM(right_factors.shape, jnp.bfloat16),
            pltpu.VMEM(tile_pattern.shape, jnp.int32),
            pltpu.VMEM((RIGHT * ROWS, 2 * LANES), jnp.bfloat16),
            pltpu.VMEM((INNER, LEFT, ROWS, LANES), jnp.float32),
            pltpu.VMEM((INNER, LEFT, ROWS, LANES), jnp.float32),
            pltpu.VMEM((GROUP, 2 * ROWS, LANES), jnp.bfloat16),
            pltpu.VMEM((GROUP, 2 * ROWS, LANES), jnp.bfloat16),
            pltpu.SemaphoreType.DMA((PAIRS,)),
            pltpu.SemaphoreType.DMA((PAIRS,)),
            pltpu.SemaphoreType.DMA((8,)),
            pltpu.SemaphoreType.DMA((8,)),
            pltpu.SemaphoreType.DMA((INNER,)),
            pltpu.SemaphoreType.DMA((INNER,)),
            pltpu.SemaphoreType.DMA((GROUP,)),
            pltpu.SemaphoreType.DMA((GROUP,)),
            pltpu.SemaphoreType.DMA((4,)),
            pltpu.SemaphoreType.REGULAR,
        ],
        compiler_params=pltpu.CompilerParams(
            collective_id=0, has_side_effects=True, vmem_limit_bytes=16 << 20
        ),
    )(*(pltpu.with_memory_space_constraint(operand, pltpu.HBM) for operand in operands))
    return ladder / (occupied_shift[:, None] + virtual_shift[None, :])


def solution(mesh):
    torus = Mesh(
        mesh.devices.reshape(PLANES, 2, 2, mesh.shape["inner"]), (*TILE_AXES, "inner")
    )
    placed = (
        P(TILE_AXES, "inner"),
        P(TILE_AXES, "inner"),
        P(None, TILE_AXES),
        P(),
        P("inner"),
        P(TILE_AXES),
    )
    return jax.shard_map(
        on_device, mesh=torus, in_specs=placed, out_specs=P("inner", TILE_AXES), check_vma=False
    )
```

```python
import jax
import jax.numpy as jnp
from jax import lax
from jax.experimental import pallas as pl
from jax.experimental.pallas import tpu as pltpu
from jax.sharding import Mesh
from jax.sharding import PartitionSpec as P

TILE = 512
TILE_AXES = ("z", "y", "core")
MESH_ID = pl.DeviceIdType.MESH
PLANES = 16
PAIRS = 8
INNER = 8
QUADS = 4
LEFT = 4
RIGHT = 128
ROWS = 8
DEPTH = 16
LANES = 128
GROUP = PLANES * QUADS
CHUNKS = 4
PER = GROUP // CHUNKS


def kernel(
    a_ref, l_ref, r_ref, pattern_ref, out_ref,
    a_all, l_all, r_all, pattern, kron, m_out, m_in, s_out, s_in,
    gather_send, gather_recv, near_send, near_recv, m_send, m_recv, s_send, s_recv, own_sem, ready,
):
    z = lax.axis_index("z")
    y = lax.axis_index("y")
    core = lax.axis_index("core")
    inner = lax.axis_index("inner")
    quad = y * 2 + core
    place = z * QUADS + quad
    pair = z // 2
    parity = z % 2

    def plane_device(plane):
        return dict(z=plane, y=y, core=core, inner=inner)

    def near_device(step):
        return dict(
            z=z,
            y=y if step == 1 else 1 - y,
            core=core if step == 2 else 1 - core,
            inner=inner,
        )

    def near_quad(step):
        return (y if step == 1 else 1 - y) * 2 + (core if step == 2 else 1 - core)

    def inner_device(other):
        return dict(z=z, y=y, core=core, inner=other)

    def tile_device(spot):
        return dict(z=spot >> 2, y=(spot >> 1) & 1, core=spot & 1, inner=inner)

    def greet(semaphore, device):
        pl.semaphore_signal(semaphore, 1, device_id=device, device_id_type=MESH_ID)

    barrier = pltpu.get_barrier_semaphore()
    for step in (4, 12, 2, 14):
        greet(barrier, plane_device((z + step) % PLANES))
    greet(barrier, plane_device(pair * 2 + 1 - parity))
    for step in (1, 2, 3):
        greet(barrier, near_device(step))
    for step in range(1, INNER):
        greet(barrier, inner_device((inner + step) % INNER))

    own_a = pltpu.make_async_copy(a_ref, a_all.at[pair], own_sem.at[0])
    own_l = pltpu.make_async_copy(l_ref, l_all.at[parity, quad], own_sem.at[1])
    own_r = pltpu.make_async_copy(r_ref, r_all, own_sem.at[2])
    own_p = pltpu.make_async_copy(pattern_ref, pattern, own_sem.at[3])
    own_a.start()
    own_l.start()
    own_p.start()
    own_r.start()
    pl.semaphore_wait(barrier, 5 + QUADS - 1 + INNER - 1)

    def factor_copy(src, side, step):
        spot = side * 4 + step
        mine = parity if side == 0 else 1 - parity
        return pltpu.make_async_remote_copy(
            src_ref=src,
            dst_ref=l_all.at[mine, quad],
            send_sem=near_send.at[spot],
            recv_sem=near_recv.at[spot],
            device_id=near_device(step) if step else plane_device(pair * 2 + 1 - parity),
            device_id_type=MESH_ID,
        )

    def factor_arrival(side, step):
        spot = side * 4 + step
        mine = parity if side == 0 else 1 - parity
        if step == 0:
            dst = l_all.at[1 - parity, quad]
        else:
            dst = l_all.at[mine, near_quad(step)]
        return pltpu.make_async_remote_copy(
            src_ref=l_ref,
            dst_ref=dst,
            send_sem=near_send.at[spot],
            recv_sem=near_recv.at[spot],
            device_id=plane_device(z),
            device_id_type=MESH_ID,
        )

    def gather_copy(slot, source, step, columns=slice(None), half=0):
        return pltpu.make_async_remote_copy(
            src_ref=(a_ref if source is pair else a_all.at[source]).at[:, columns],
            dst_ref=a_all.at[source, :, columns],
            send_sem=gather_send.at[slot],
            recv_sem=gather_recv.at[source, half],
            device_id=plane_device((pair + step) % PAIRS * 2 + parity),
            device_id_type=MESH_ID,
        )

    def gather_arrival(source, columns=slice(None), half=0):
        return pltpu.make_async_remote_copy(
            src_ref=a_ref.at[:, columns],
            dst_ref=a_all.at[source, :, columns],
            send_sem=gather_send.at[0],
            recv_sem=gather_recv.at[source, half],
            device_id=plane_device(z),
            device_id_type=MESH_ID,
        )

    width = a_ref.shape[1] // 2
    halves = [pl.ds(half * width, width) for half in range(2)]

    shared = [factor_copy(l_ref, 0, step) for step in range(4)]
    first = [
        gather_copy(side * 2 + half, pair, step, halves[half], half)
        for half in range(2)
        for side, step in enumerate((2, 6))
    ]
    second = [gather_copy(4 + side, pair, step) for side, step in enumerate((1, 7))]
    for copy in first + shared + second:
        copy.start()
    gathered = first + second
    own_p.wait()
    mask = jnp.where(pattern[...] != 0, 1.0, 0.0).astype(jnp.bfloat16)
    spread = jnp.where(
        lax.broadcasted_iota(jnp.int32, (32, 256), 0)
        == lax.broadcasted_iota(jnp.int32, (32, 256), 1) >> 3,
        1.0,
        0.0,
    ).astype(jnp.bfloat16)
    spread = lax.dot_general(
        mask, spread, (((0,), (0,)), ((), ())), preferred_element_type=jnp.float32
    ).astype(jnp.bfloat16)
    same = jnp.where(
        (lax.broadcasted_iota(jnp.int32, (LANES, 256), 0) & 7)
        == (lax.broadcasted_iota(jnp.int32, (LANES, 256), 1) & 7),
        1.0,
        0.0,
    )
    lifted = lax.broadcasted_iota(jnp.int32, (LANES, RIGHT), 1) - (
        lax.broadcasted_iota(jnp.int32, (LANES, RIGHT), 0) >> 3
    )

    @pl.loop(0, RIGHT // 16)
    def _(block):
        lift = jnp.where(lifted == block * 16, 1.0, 0.0).astype(jnp.bfloat16)
        rows = jnp.dot(lift, spread, preferred_element_type=jnp.float32)
        kron[pl.ds(pl.multiple_of(block * LANES, LANES), LANES), :] = (rows * same).astype(
            jnp.bfloat16
        )

    factor_arrival(0, 0).wait_recv()
    passed = [factor_copy(l_all.at[1 - parity, quad], 1, step) for step in (1, 2, 3)]
    for copy in passed:
        copy.start()
    for half in range(2):
        for side, (back, on, over) in enumerate(((6, 1, 2), (2, 7, 6))):
            source = (pair + back) % PAIRS
            gather_arrival(source, halves[half], half).wait_recv()
            onward = [gather_copy(6 + side * 2 + half, source, on, halves[half], half)]
            if half == side:
                onward.append(gather_copy(10 + side, source, over, halves[half], half))
            for copy in onward:
                copy.start()
            gathered.extend(onward)
    own_a.wait()
    own_l.wait()
    for side in range(2):
        for step in (1, 2, 3):
            factor_arrival(side, step).wait_recv()

    def mix_copy(other):
        return pltpu.make_async_remote_copy(
            src_ref=m_out.at[other],
            dst_ref=m_in.at[inner],
            send_sem=m_send.at[other],
            recv_sem=m_recv.at[inner],
            device_id=inner_device(other),
            device_id_type=MESH_ID,
        )

    def mix_arrival(other):
        return pltpu.make_async_remote_copy(
            src_ref=m_out.at[other],
            dst_ref=m_in.at[other],
            send_sem=m_send.at[other],
            recv_sem=m_recv.at[other],
            device_id=inner_device(other),
            device_id_type=MESH_ID,
        )

    def tile_copy(spot):
        return pltpu.make_async_remote_copy(
            src_ref=s_out.at[spot],
            dst_ref=s_in.at[place],
            send_sem=s_send.at[spot],
            recv_sem=s_recv.at[place],
            device_id=tile_device(spot),
            device_id_type=MESH_ID,
        )

    def tile_arrival(spot):
        return pltpu.make_async_remote_copy(
            src_ref=s_out.at[spot],
            dst_ref=s_in.at[spot],
            send_sem=s_send.at[spot],
            recv_sem=s_recv.at[spot],
            device_id=tile_device(spot),
            device_id_type=MESH_ID,
        )

    for step in (0, 2, 6, 1, 7, 3, 5, 4):
        other = (pair + step) % PAIRS
        if step in (3, 4, 5):
            for half in range(2):
                gather_arrival(other, halves[half], half).wait_recv()
        elif step in (1, 7):
            gather_arrival(other).wait_recv()
        for left in range(LEFT):
            columns = pl.ds(left * TILE, TILE)
            m_out[other, left] = lax.dot_general(
                a_all[other, :, columns],
                l_all[:, :, :, columns].reshape(LANES, TILE),
                (((1,), (1,)), ((), ())),
                preferred_element_type=jnp.float32,
            )

        @pl.when(other != inner)
        def _(other=other):
            mix_copy(other).start()

    for step in (1, 2, 3):
        greet(ready, near_device(step))
    m_in[inner] = m_out[inner]
    pl.semaphore_wait(ready, QUADS - 1)

    @pl.loop(1, INNER)
    def _(step):
        mix_arrival((inner + step) % INNER).wait_recv()

    stacked = m_in[...].reshape(INNER * LEFT * ROWS, LANES)
    high = stacked.astype(jnp.bfloat16)
    low = (stacked - high.astype(jnp.float32)).astype(jnp.bfloat16)
    split = jnp.concatenate([high, low], axis=1)
    for chunk in range(CHUNKS):
        rows = pl.ds(chunk * PER * 2 * ROWS, PER * 2 * ROWS)
        both = jnp.dot(kron[rows, :], split, preferred_element_type=jnp.float32)
        both = both[:, :LANES] + both[:, LANES:]
        s_out[pl.ds(chunk * PER, PER)] = both.astype(jnp.bfloat16).reshape(PER, 2 * ROWS, LANES)

    @pl.loop(0, PLANES)
    def _(count):
        plane = (count & 8) + ((z + count) & 7)

        @pl.when(plane != z)
        def _():
            for turned in range(QUADS):
                tile_copy(plane * QUADS + (quad ^ turned)).start()

        @pl.when(plane == z)
        def _():
            for turned in range(1, QUADS):
                tile_copy(plane * QUADS + (quad ^ turned)).start()

    s_in[place] = s_out[place]

    own_r.wait()

    @pl.loop(1, GROUP)
    def _(step):
        tile_arrival((place + step) & (GROUP - 1)).wait_recv()

    mixed = jnp.concatenate(
        [s_in[pl.ds(eight * 8, 8)].reshape(LANES, LANES) for eight in range(GROUP // 8)], axis=1
    )
    for side in range(2):
        columns = pl.ds(side * TILE, TILE)
        ladder = jnp.dot(mixed, r_all[:, columns], preferred_element_type=jnp.float32)
        ladder = ladder.reshape(8, 2, ROWS, TILE)[:, side]
        out_ref[:, columns] = ladder.reshape(8 * ROWS, TILE)

    for copy in shared + passed + gathered:
        copy.wait_send()

    @pl.loop(1, INNER)
    def _(step):
        mix_arrival((inner + step) % INNER).wait_send()

    @pl.loop(1, GROUP)
    def _(step):
        tile_arrival((place + step) & (GROUP - 1)).wait_send()


def on_device(amplitudes, left_factors, right_factors, tile_pattern, occupied_shift, virtual_shift):
    width = amplitudes.shape[1]
    out_width = right_factors.shape[1]
    operands = (amplitudes, left_factors, right_factors, tile_pattern)
    ladder = pl.pallas_call(
        kernel,
        name="ladder",
        out_shape=jax.ShapeDtypeStruct((occupied_shift.shape[0], out_width), jnp.float32),
        in_specs=[pl.BlockSpec(memory_space=pltpu.HBM)] * 4,
        out_specs=pl.BlockSpec(memory_space=pltpu.VMEM),
        scratch_shapes=[
            pltpu.VMEM((PAIRS, ROWS, width), jnp.bfloat16),
            pltpu.VMEM((2, QUADS, DEPTH, width), jnp.bfloat16),
            pltpu.VMEM(right_factors.shape, jnp.bfloat16),
            pltpu.VMEM(tile_pattern.shape, jnp.int32),
            pltpu.VMEM((RIGHT * ROWS, 2 * LANES), jnp.bfloat16),
            pltpu.VMEM((INNER, LEFT, ROWS, LANES), jnp.float32),
            pltpu.VMEM((INNER, LEFT, ROWS, LANES), jnp.float32),
            pltpu.VMEM((GROUP, 2 * ROWS, LANES), jnp.bfloat16),
            pltpu.VMEM((GROUP, 2 * ROWS, LANES), jnp.bfloat16),
            pltpu.SemaphoreType.DMA((12,)),
            pltpu.SemaphoreType.DMA((PAIRS, 2)),
            pltpu.SemaphoreType.DMA((8,)),
            pltpu.SemaphoreType.DMA((8,)),
            pltpu.SemaphoreType.DMA((INNER,)),
            pltpu.SemaphoreType.DMA((INNER,)),
            pltpu.SemaphoreType.DMA((GROUP,)),
            pltpu.SemaphoreType.DMA((GROUP,)),
            pltpu.SemaphoreType.DMA((4,)),
            pltpu.SemaphoreType.REGULAR,
        ],
        compiler_params=pltpu.CompilerParams(
            collective_id=0, has_side_effects=True, vmem_limit_bytes=16 << 20
        ),
    )(*(pltpu.with_memory_space_constraint(operand, pltpu.HBM) for operand in operands))
    return ladder / (occupied_shift[:, None] + virtual_shift[None, :])


def solution(mesh):
    torus = Mesh(
        mesh.devices.reshape(PLANES, 2, 2, mesh.shape["inner"]), (*TILE_AXES, "inner")
    )
    placed = (
        P(TILE_AXES, "inner"),
        P(TILE_AXES, "inner"),
        P(None, TILE_AXES),
        P(),
        P("inner"),
        P(TILE_AXES),
    )
    return jax.shard_map(
        on_device, mesh=torus, in_specs=placed, out_specs=P("inner", TILE_AXES), check_vma=False
    )
```

```python
import jax
import jax.numpy as jnp
from jax import lax
from jax.experimental import pallas as pl
from jax.experimental.pallas import tpu as pltpu
from jax.sharding import Mesh
from jax.sharding import PartitionSpec as P

TILE = 512
TILE_AXES = ("z", "y", "core")
MESH_ID = pl.DeviceIdType.MESH
PLANES = 16
PAIRS = 8
INNER = 8
QUADS = 4
LEFT = 4
RIGHT = 128
ROWS = 8
DEPTH = 16
LANES = 128
GROUP = PLANES * QUADS
CHUNKS = 4
PER = GROUP // CHUNKS


def kernel(
    a_ref, l_ref, r_ref, pattern_ref, out_ref,
    a_all, l_all, r_all, pattern, kron, m_out, m_in, s_out, s_in,
    gather_send, gather_recv, near_send, near_recv, m_send, m_recv, s_send, s_recv, own_sem, ready,
):
    z = lax.axis_index("z")
    y = lax.axis_index("y")
    core = lax.axis_index("core")
    inner = lax.axis_index("inner")
    quad = y * 2 + core
    place = z * QUADS + quad
    pair = z // 2
    parity = z % 2

    def plane_device(plane):
        return dict(z=plane, y=y, core=core, inner=inner)

    def near_device(step):
        return dict(
            z=z,
            y=y if step == 1 else 1 - y,
            core=core if step == 2 else 1 - core,
            inner=inner,
        )

    def near_quad(step):
        return (y if step == 1 else 1 - y) * 2 + (core if step == 2 else 1 - core)

    def inner_device(other):
        return dict(z=z, y=y, core=core, inner=other)

    def tile_device(spot):
        return dict(z=spot >> 2, y=(spot >> 1) & 1, core=spot & 1, inner=inner)

    def greet(semaphore, device):
        pl.semaphore_signal(semaphore, 1, device_id=device, device_id_type=MESH_ID)

    barrier = pltpu.get_barrier_semaphore()
    for step in (4, 12, 2, 14):
        greet(barrier, plane_device((z + step) % PLANES))
    greet(barrier, plane_device(pair * 2 + 1 - parity))
    for step in (1, 2, 3):
        greet(barrier, near_device(step))
    for step in range(1, INNER):
        greet(barrier, inner_device((inner + step) % INNER))

    own_a = pltpu.make_async_copy(a_ref, a_all.at[pair], own_sem.at[0])
    own_l = pltpu.make_async_copy(l_ref, l_all.at[parity, quad], own_sem.at[1])
    own_r = pltpu.make_async_copy(r_ref, r_all, own_sem.at[2])
    own_p = pltpu.make_async_copy(pattern_ref, pattern, own_sem.at[3])
    own_a.start()
    own_l.start()
    own_p.start()
    own_r.start()
    own_p.wait()
    mask = jnp.where(pattern[...] != 0, 1.0, 0.0).astype(jnp.bfloat16)
    spread = jnp.where(
        lax.broadcasted_iota(jnp.int32, (32, 256), 0)
        == lax.broadcasted_iota(jnp.int32, (32, 256), 1) >> 3,
        1.0,
        0.0,
    ).astype(jnp.bfloat16)
    spread = lax.dot_general(
        mask, spread, (((0,), (0,)), ((), ())), preferred_element_type=jnp.float32
    ).astype(jnp.bfloat16)
    same = jnp.where(
        (lax.broadcasted_iota(jnp.int32, (LANES, 256), 0) & 7)
        == (lax.broadcasted_iota(jnp.int32, (LANES, 256), 1) & 7),
        1.0,
        0.0,
    )
    lifted = lax.broadcasted_iota(jnp.int32, (LANES, RIGHT), 1) - (
        lax.broadcasted_iota(jnp.int32, (LANES, RIGHT), 0) >> 3
    )

    @pl.loop(0, RIGHT // 16)
    def _(block):
        lift = jnp.where(lifted == block * 16, 1.0, 0.0).astype(jnp.bfloat16)
        rows = jnp.dot(lift, spread, preferred_element_type=jnp.float32)
        kron[pl.ds(pl.multiple_of(block * LANES, LANES), LANES), :] = (rows * same).astype(
            jnp.bfloat16
        )

    pl.semaphore_wait(barrier, 5 + QUADS - 1 + INNER - 1)

    def factor_copy(src, side, step):
        spot = side * 4 + step
        mine = parity if side == 0 else 1 - parity
        return pltpu.make_async_remote_copy(
            src_ref=src,
            dst_ref=l_all.at[mine, quad],
            send_sem=near_send.at[spot],
            recv_sem=near_recv.at[spot],
            device_id=near_device(step) if step else plane_device(pair * 2 + 1 - parity),
            device_id_type=MESH_ID,
        )

    def factor_arrival(side, step):
        spot = side * 4 + step
        mine = parity if side == 0 else 1 - parity
        if step == 0:
            dst = l_all.at[1 - parity, quad]
        else:
            dst = l_all.at[mine, near_quad(step)]
        return pltpu.make_async_remote_copy(
            src_ref=l_ref,
            dst_ref=dst,
            send_sem=near_send.at[spot],
            recv_sem=near_recv.at[spot],
            device_id=plane_device(z),
            device_id_type=MESH_ID,
        )

    def gather_copy(slot, source, step, columns=slice(None), half=0):
        return pltpu.make_async_remote_copy(
            src_ref=(a_ref if source is pair else a_all.at[source]).at[:, columns],
            dst_ref=a_all.at[source, :, columns],
            send_sem=gather_send.at[slot],
            recv_sem=gather_recv.at[source, half],
            device_id=plane_device((pair + step) % PAIRS * 2 + parity),
            device_id_type=MESH_ID,
        )

    def gather_arrival(source, columns=slice(None), half=0):
        return pltpu.make_async_remote_copy(
            src_ref=a_ref.at[:, columns],
            dst_ref=a_all.at[source, :, columns],
            send_sem=gather_send.at[0],
            recv_sem=gather_recv.at[source, half],
            device_id=plane_device(z),
            device_id_type=MESH_ID,
        )

    width = a_ref.shape[1] // 2
    halves = [pl.ds(half * width, width) for half in range(2)]

    shared = [factor_copy(l_ref, 0, step) for step in range(4)]
    first = [
        gather_copy(side * 2 + half, pair, step, halves[half], half)
        for half in range(2)
        for side, step in enumerate((2, 6))
    ]
    second = [gather_copy(4 + side, pair, step) for side, step in enumerate((1, 7))]
    for copy in first + shared + second:
        copy.start()
    gathered = first + second
    factor_arrival(0, 0).wait_recv()
    passed = [factor_copy(l_all.at[1 - parity, quad], 1, step) for step in (1, 2, 3)]
    for copy in passed:
        copy.start()
    for half in range(2):
        for side, (back, on, over) in enumerate(((6, 1, 2), (2, 7, 6))):
            source = (pair + back) % PAIRS
            gather_arrival(source, halves[half], half).wait_recv()
            onward = [gather_copy(6 + side * 2 + half, source, on, halves[half], half)]
            for copy in onward:
                copy.start()
            gathered.extend(onward)
    for side, (back, over) in enumerate(((5, 1), (3, 7))):
        source = (pair + back) % PAIRS
        gather_arrival(source, halves[side], side).wait_recv()
        onward = gather_copy(10 + side, source, over, halves[side], side)
        onward.start()
        gathered.append(onward)

    own_a.wait()
    own_l.wait()
    for side in range(2):
        for step in (1, 2, 3):
            factor_arrival(side, step).wait_recv()

    def mix_copy(other):
        return pltpu.make_async_remote_copy(
            src_ref=m_out.at[other],
            dst_ref=m_in.at[inner],
            send_sem=m_send.at[other],
            recv_sem=m_recv.at[inner],
            device_id=inner_device(other),
            device_id_type=MESH_ID,
        )

    def mix_arrival(other):
        return pltpu.make_async_remote_copy(
            src_ref=m_out.at[other],
            dst_ref=m_in.at[other],
            send_sem=m_send.at[other],
            recv_sem=m_recv.at[other],
            device_id=inner_device(other),
            device_id_type=MESH_ID,
        )

    def tile_copy(spot):
        return pltpu.make_async_remote_copy(
            src_ref=s_out.at[spot],
            dst_ref=s_in.at[place],
            send_sem=s_send.at[spot],
            recv_sem=s_recv.at[place],
            device_id=tile_device(spot),
            device_id_type=MESH_ID,
        )

    def tile_arrival(spot):
        return pltpu.make_async_remote_copy(
            src_ref=s_out.at[spot],
            dst_ref=s_in.at[spot],
            send_sem=s_send.at[spot],
            recv_sem=s_recv.at[spot],
            device_id=tile_device(spot),
            device_id_type=MESH_ID,
        )

    for step in (0, 2, 6, 1, 7, 3, 5, 4):
        other = (pair + step) % PAIRS
        if step in (3, 4, 5):
            for half in ((0, 1) if step == 4 else (0,) if step == 3 else (1,)):
                gather_arrival(other, halves[half], half).wait_recv()
        elif step in (1, 7):
            gather_arrival(other).wait_recv()
        for left in range(LEFT):
            columns = pl.ds(left * TILE, TILE)
            m_out[other, left] = lax.dot_general(
                a_all[other, :, columns],
                l_all[:, :, :, columns].reshape(LANES, TILE),
                (((1,), (1,)), ((), ())),
                preferred_element_type=jnp.float32,
            )

        @pl.when(other != inner)
        def _(other=other):
            mix_copy(other).start()

    for step in (1, 2, 3):
        greet(ready, near_device(step))
    m_in[inner] = m_out[inner]
    pl.semaphore_wait(ready, QUADS - 1)

    @pl.loop(1, INNER)
    def _(step):
        mix_arrival((inner + step) % INNER).wait_recv()

    stacked = m_in[...].reshape(INNER * LEFT * ROWS, LANES)
    high = stacked.astype(jnp.bfloat16)
    low = (stacked - high.astype(jnp.float32)).astype(jnp.bfloat16)
    split = jnp.concatenate([high, low], axis=1)
    for chunk in range(CHUNKS):
        rows = pl.ds(chunk * PER * 2 * ROWS, PER * 2 * ROWS)
        both = jnp.dot(kron[rows, :], split, preferred_element_type=jnp.float32)
        both = both[:, :LANES] + both[:, LANES:]
        s_out[pl.ds(chunk * PER, PER)] = both.astype(jnp.bfloat16).reshape(PER, 2 * ROWS, LANES)

    @pl.loop(0, PLANES)
    def _(count):
        plane = (count & 8) + ((z + count) & 7)

        @pl.when(plane != z)
        def _():
            for turned in range(QUADS):
                tile_copy(plane * QUADS + (quad ^ turned)).start()

        @pl.when(plane == z)
        def _():
            for turned in range(1, QUADS):
                tile_copy(plane * QUADS + (quad ^ turned)).start()

    s_in[place] = s_out[place]

    own_r.wait()

    @pl.loop(1, GROUP)
    def _(step):
        tile_arrival((place + step) & (GROUP - 1)).wait_recv()

    mixed = jnp.concatenate(
        [s_in[pl.ds(eight * 8, 8)].reshape(LANES, LANES) for eight in range(GROUP // 8)], axis=1
    )
    for side in range(2):
        columns = pl.ds(side * TILE, TILE)
        ladder = jnp.dot(mixed, r_all[:, columns], preferred_element_type=jnp.float32)
        ladder = ladder.reshape(8, 2, ROWS, TILE)[:, side]
        out_ref[:, columns] = ladder.reshape(8 * ROWS, TILE)

    for copy in shared + passed + gathered:
        copy.wait_send()

    @pl.loop(1, INNER)
    def _(step):
        mix_arrival((inner + step) % INNER).wait_send()

    @pl.loop(1, GROUP)
    def _(step):
        tile_arrival((place + step) & (GROUP - 1)).wait_send()


def on_device(amplitudes, left_factors, right_factors, tile_pattern, occupied_shift, virtual_shift):
    width = amplitudes.shape[1]
    out_width = right_factors.shape[1]
    operands = (amplitudes, left_factors, right_factors, tile_pattern)
    ladder = pl.pallas_call(
        kernel,
        name="ladder",
        out_shape=jax.ShapeDtypeStruct((occupied_shift.shape[0], out_width), jnp.float32),
        in_specs=[pl.BlockSpec(memory_space=pltpu.HBM)] * 4,
        out_specs=pl.BlockSpec(memory_space=pltpu.VMEM),
        scratch_shapes=[
            pltpu.VMEM((PAIRS, ROWS, width), jnp.bfloat16),
            pltpu.VMEM((2, QUADS, DEPTH, width), jnp.bfloat16),
            pltpu.VMEM(right_factors.shape, jnp.bfloat16),
            pltpu.VMEM(tile_pattern.shape, jnp.int32),
            pltpu.VMEM((RIGHT * ROWS, 2 * LANES), jnp.bfloat16),
            pltpu.VMEM((INNER, LEFT, ROWS, LANES), jnp.float32),
            pltpu.VMEM((INNER, LEFT, ROWS, LANES), jnp.float32),
            pltpu.VMEM((GROUP, 2 * ROWS, LANES), jnp.bfloat16),
            pltpu.VMEM((GROUP, 2 * ROWS, LANES), jnp.bfloat16),
            pltpu.SemaphoreType.DMA((12,)),
            pltpu.SemaphoreType.DMA((PAIRS, 2)),
            pltpu.SemaphoreType.DMA((8,)),
            pltpu.SemaphoreType.DMA((8,)),
            pltpu.SemaphoreType.DMA((INNER,)),
            pltpu.SemaphoreType.DMA((INNER,)),
            pltpu.SemaphoreType.DMA((GROUP,)),
            pltpu.SemaphoreType.DMA((GROUP,)),
            pltpu.SemaphoreType.DMA((4,)),
            pltpu.SemaphoreType.REGULAR,
        ],
        compiler_params=pltpu.CompilerParams(
            collective_id=0, has_side_effects=True, vmem_limit_bytes=16 << 20
        ),
    )(*(pltpu.with_memory_space_constraint(operand, pltpu.HBM) for operand in operands))
    return ladder / (occupied_shift[:, None] + virtual_shift[None, :])


def solution(mesh):
    torus = Mesh(
        mesh.devices.reshape(PLANES, 2, 2, mesh.shape["inner"]), (*TILE_AXES, "inner")
    )
    placed = (
        P(TILE_AXES, "inner"),
        P(TILE_AXES, "inner"),
        P(None, TILE_AXES),
        P(),
        P("inner"),
        P(TILE_AXES),
    )
    return jax.shard_map(
        on_device, mesh=torus, in_specs=placed, out_specs=P("inner", TILE_AXES), check_vma=False
    )
```

```python
import jax
import jax.numpy as jnp
from jax import lax
from jax.experimental import pallas as pl
from jax.experimental.pallas import tpu as pltpu
from jax.sharding import Mesh
from jax.sharding import PartitionSpec as P

TILE = 512
TILE_AXES = ("z", "y", "core")
MESH_ID = pl.DeviceIdType.MESH
PLANES = 16
PAIRS = 8
INNER = 8
QUADS = 4
LEFT = 4
RIGHT = 128
ROWS = 8
DEPTH = 16
LANES = 128
GROUP = PLANES * QUADS
CHUNKS = 4
PER = GROUP // CHUNKS


def kernel(
    a_ref, l_ref, r_ref, pattern_ref, out_ref,
    a_all, l_all, r_all, pattern, kron, m_out, m_in, s_out, s_in,
    gather_send, gather_recv, near_send, near_recv, m_send, m_recv, s_send, s_recv, own_sem, ready,
):
    z = lax.axis_index("z")
    y = lax.axis_index("y")
    core = lax.axis_index("core")
    inner = lax.axis_index("inner")
    quad = y * 2 + core
    place = z * QUADS + quad
    pair = z // 2
    parity = z % 2

    def plane_device(plane):
        return dict(z=plane, y=y, core=core, inner=inner)

    def near_device(step):
        return dict(
            z=z,
            y=y if step == 1 else 1 - y,
            core=core if step == 2 else 1 - core,
            inner=inner,
        )

    def near_quad(step):
        return (y if step == 1 else 1 - y) * 2 + (core if step == 2 else 1 - core)

    def inner_device(other):
        return dict(z=z, y=y, core=core, inner=other)

    def tile_device(spot):
        return dict(z=spot >> 2, y=(spot >> 1) & 1, core=spot & 1, inner=inner)

    def greet(semaphore, device):
        pl.semaphore_signal(semaphore, 1, device_id=device, device_id_type=MESH_ID)

    barrier = pltpu.get_barrier_semaphore()
    for step in (4, 12, 2, 14):
        greet(barrier, plane_device((z + step) % PLANES))
    greet(barrier, plane_device(pair * 2 + 1 - parity))
    for step in (1, 2, 3):
        greet(barrier, near_device(step))
    for step in range(1, INNER):
        greet(barrier, inner_device((inner + step) % INNER))

    own_a = pltpu.make_async_copy(a_ref, a_all.at[pair], own_sem.at[0])
    own_l = pltpu.make_async_copy(l_ref, l_all.at[parity, quad], own_sem.at[1])
    own_r = pltpu.make_async_copy(r_ref, r_all, own_sem.at[2])
    own_p = pltpu.make_async_copy(pattern_ref, pattern, own_sem.at[3])
    own_a.start()
    own_l.start()
    own_p.start()
    own_r.start()
    own_p.wait()
    mask = jnp.where(pattern[...] != 0, 1.0, 0.0).astype(jnp.bfloat16)
    spread = jnp.where(
        lax.broadcasted_iota(jnp.int32, (32, 256), 0)
        == lax.broadcasted_iota(jnp.int32, (32, 256), 1) >> 3,
        1.0,
        0.0,
    ).astype(jnp.bfloat16)
    spread = lax.dot_general(
        mask, spread, (((0,), (0,)), ((), ())), preferred_element_type=jnp.float32
    ).astype(jnp.bfloat16)
    same = jnp.where(
        (lax.broadcasted_iota(jnp.int32, (LANES, 256), 0) & 7)
        == (lax.broadcasted_iota(jnp.int32, (LANES, 256), 1) & 7),
        1.0,
        0.0,
    )
    lifted = lax.broadcasted_iota(jnp.int32, (LANES, RIGHT), 1) - (
        lax.broadcasted_iota(jnp.int32, (LANES, RIGHT), 0) >> 3
    )

    @pl.loop(0, RIGHT // 16)
    def _(block):
        lift = jnp.where(lifted == block * 16, 1.0, 0.0).astype(jnp.bfloat16)
        rows = jnp.dot(lift, spread, preferred_element_type=jnp.float32)
        kron[pl.ds(pl.multiple_of(block * LANES, LANES), LANES), :] = (rows * same).astype(
            jnp.bfloat16
        )

    pl.semaphore_wait(barrier, 5 + QUADS - 1 + INNER - 1)

    def factor_copy(src, side, step):
        spot = side * 4 + step
        mine = parity if side == 0 else 1 - parity
        return pltpu.make_async_remote_copy(
            src_ref=src,
            dst_ref=l_all.at[mine, quad],
            send_sem=near_send.at[spot],
            recv_sem=near_recv.at[spot],
            device_id=near_device(step) if step else plane_device(pair * 2 + 1 - parity),
            device_id_type=MESH_ID,
        )

    def factor_arrival(side, step):
        spot = side * 4 + step
        mine = parity if side == 0 else 1 - parity
        if step == 0:
            dst = l_all.at[1 - parity, quad]
        else:
            dst = l_all.at[mine, near_quad(step)]
        return pltpu.make_async_remote_copy(
            src_ref=l_ref,
            dst_ref=dst,
            send_sem=near_send.at[spot],
            recv_sem=near_recv.at[spot],
            device_id=plane_device(z),
            device_id_type=MESH_ID,
        )

    def gather_copy(slot, source, step, columns=slice(None), half=0):
        return pltpu.make_async_remote_copy(
            src_ref=(a_ref if source is pair else a_all.at[source]).at[:, columns],
            dst_ref=a_all.at[source, :, columns],
            send_sem=gather_send.at[slot],
            recv_sem=gather_recv.at[source, half],
            device_id=plane_device((pair + step) % PAIRS * 2 + parity),
            device_id_type=MESH_ID,
        )

    def gather_arrival(source, columns=slice(None), half=0):
        return pltpu.make_async_remote_copy(
            src_ref=a_ref.at[:, columns],
            dst_ref=a_all.at[source, :, columns],
            send_sem=gather_send.at[0],
            recv_sem=gather_recv.at[source, half],
            device_id=plane_device(z),
            device_id_type=MESH_ID,
        )

    width = a_ref.shape[1] // 2
    halves = [pl.ds(half * width, width) for half in range(2)]

    shared = [factor_copy(l_ref, 0, step) for step in range(4)]
    first = [
        gather_copy(side * 2 + half, pair, step, halves[half], half)
        for half in range(2)
        for side, step in enumerate((2, 6))
    ]
    second = [gather_copy(4 + side, pair, step) for side, step in enumerate((1, 7))]
    for copy in first + shared + second:
        copy.start()
    gathered = first + second
    factor_arrival(0, 0).wait_recv()
    passed = [factor_copy(l_all.at[1 - parity, quad], 1, step) for step in (1, 2, 3)]
    for copy in passed:
        copy.start()
    for half in range(2):
        for side, (back, on, over) in enumerate(((6, 1, 2), (2, 7, 6))):
            source = (pair + back) % PAIRS
            gather_arrival(source, halves[half], half).wait_recv()
            onward = [gather_copy(6 + side * 2 + half, source, on, halves[half], half)]
            for copy in onward:
                copy.start()
            gathered.extend(onward)
    for side, (back, over) in enumerate(((5, 1), (3, 7))):
        source = (pair + back) % PAIRS
        gather_arrival(source, halves[side], side).wait_recv()
        onward = gather_copy(10 + side, source, over, halves[side], side)
        onward.start()
        gathered.append(onward)

    own_a.wait()
    own_l.wait()
    for side in range(2):
        for step in (1, 2, 3):
            factor_arrival(side, step).wait_recv()

    def mix_copy(other):
        return pltpu.make_async_remote_copy(
            src_ref=m_out.at[other],
            dst_ref=m_in.at[inner],
            send_sem=m_send.at[other],
            recv_sem=m_recv.at[inner],
            device_id=inner_device(other),
            device_id_type=MESH_ID,
        )

    def mix_arrival(other):
        return pltpu.make_async_remote_copy(
            src_ref=m_out.at[other],
            dst_ref=m_in.at[other],
            send_sem=m_send.at[other],
            recv_sem=m_recv.at[other],
            device_id=inner_device(other),
            device_id_type=MESH_ID,
        )

    def tile_copy(spot):
        return pltpu.make_async_remote_copy(
            src_ref=s_out.at[spot],
            dst_ref=s_in.at[place],
            send_sem=s_send.at[spot],
            recv_sem=s_recv.at[place],
            device_id=tile_device(spot),
            device_id_type=MESH_ID,
        )

    def tile_arrival(spot):
        return pltpu.make_async_remote_copy(
            src_ref=s_out.at[spot],
            dst_ref=s_in.at[spot],
            send_sem=s_send.at[spot],
            recv_sem=s_recv.at[spot],
            device_id=tile_device(spot),
            device_id_type=MESH_ID,
        )

    for step in (0, 2, 6, 1, 7, 3, 5, 4):
        other = (pair + step) % PAIRS
        if step in (3, 4, 5):
            for half in ((0, 1) if step == 4 else (0,) if step == 3 else (1,)):
                gather_arrival(other, halves[half], half).wait_recv()
        elif step in (1, 7):
            gather_arrival(other).wait_recv()
        for left in range(LEFT):
            columns = pl.ds(left * TILE, TILE)
            m_out[other, left] = lax.dot_general(
                a_all[other, :, columns],
                l_all[:, :, :, columns].reshape(LANES, TILE),
                (((1,), (1,)), ((), ())),
                preferred_element_type=jnp.float32,
            )

        @pl.when(other != inner)
        def _(other=other):
            mix_copy(other).start()

    for step in (1, 2, 3):
        greet(ready, near_device(step))
    m_in[inner] = m_out[inner]
    pl.semaphore_wait(ready, QUADS - 1)

    @pl.loop(1, INNER)
    def _(step):
        mix_arrival((inner + step) % INNER).wait_recv()

    stacked = m_in[...].reshape(INNER * LEFT * ROWS, LANES)
    high = stacked.astype(jnp.bfloat16)
    low = (stacked - high.astype(jnp.float32)).astype(jnp.bfloat16)
    split = jnp.concatenate([high, low], axis=1)
    for chunk in range(CHUNKS):
        rows = pl.ds(chunk * PER * 2 * ROWS, PER * 2 * ROWS)
        both = jnp.dot(kron[rows, :], split, preferred_element_type=jnp.float32)
        both = both[:, :LANES] + both[:, LANES:]
        s_out[pl.ds(chunk * PER, PER)] = both.astype(jnp.bfloat16).reshape(PER, 2 * ROWS, LANES)

    @pl.loop(0, PLANES)
    def _(count):
        plane = (count & 8) + ((z + count) & 7)

        @pl.when(plane != z)
        def _():
            for turned in range(QUADS):
                tile_copy(plane * QUADS + (quad ^ turned)).start()

        @pl.when(plane == z)
        def _():
            for turned in range(1, QUADS):
                tile_copy(plane * QUADS + (quad ^ turned)).start()

    s_in[place] = s_out[place]

    own_r.wait()

    span = GROUP // 2
    for part in range(2):

        @pl.loop(part * span, part * span + span)
        def _(spot):
            @pl.when(spot != place)
            def _():
                tile_arrival(spot).wait_recv()

        mixed = jnp.concatenate(
            [s_in[pl.ds(part * span + eight * 8, 8)].reshape(LANES, LANES) for eight in range(span // 8)],
            axis=1,
        )
        depths = pl.ds(part * TILE, TILE)
        for side in range(2):
            columns = pl.ds(side * TILE, TILE)
            ladder = jnp.dot(mixed, r_all[depths, columns], preferred_element_type=jnp.float32)
            ladder = ladder.reshape(8, 2, ROWS, TILE)[:, side].reshape(8 * ROWS, TILE)
            out_ref[:, columns] = ladder if part == 0 else out_ref[:, columns] + ladder

    for copy in shared + passed + gathered:
        copy.wait_send()

    @pl.loop(1, INNER)
    def _(step):
        mix_arrival((inner + step) % INNER).wait_send()

    @pl.loop(1, GROUP)
    def _(step):
        tile_arrival((place + step) & (GROUP - 1)).wait_send()


def on_device(amplitudes, left_factors, right_factors, tile_pattern, occupied_shift, virtual_shift):
    width = amplitudes.shape[1]
    out_width = right_factors.shape[1]
    operands = (amplitudes, left_factors, right_factors, tile_pattern)
    ladder = pl.pallas_call(
        kernel,
        name="ladder",
        out_shape=jax.ShapeDtypeStruct((occupied_shift.shape[0], out_width), jnp.float32),
        in_specs=[pl.BlockSpec(memory_space=pltpu.HBM)] * 4,
        out_specs=pl.BlockSpec(memory_space=pltpu.VMEM),
        scratch_shapes=[
            pltpu.VMEM((PAIRS, ROWS, width), jnp.bfloat16),
            pltpu.VMEM((2, QUADS, DEPTH, width), jnp.bfloat16),
            pltpu.VMEM(right_factors.shape, jnp.bfloat16),
            pltpu.VMEM(tile_pattern.shape, jnp.int32),
            pltpu.VMEM((RIGHT * ROWS, 2 * LANES), jnp.bfloat16),
            pltpu.VMEM((INNER, LEFT, ROWS, LANES), jnp.float32),
            pltpu.VMEM((INNER, LEFT, ROWS, LANES), jnp.float32),
            pltpu.VMEM((GROUP, 2 * ROWS, LANES), jnp.bfloat16),
            pltpu.VMEM((GROUP, 2 * ROWS, LANES), jnp.bfloat16),
            pltpu.SemaphoreType.DMA((12,)),
            pltpu.SemaphoreType.DMA((PAIRS, 2)),
            pltpu.SemaphoreType.DMA((8,)),
            pltpu.SemaphoreType.DMA((8,)),
            pltpu.SemaphoreType.DMA((INNER,)),
            pltpu.SemaphoreType.DMA((INNER,)),
            pltpu.SemaphoreType.DMA((GROUP,)),
            pltpu.SemaphoreType.DMA((GROUP,)),
            pltpu.SemaphoreType.DMA((4,)),
            pltpu.SemaphoreType.REGULAR,
        ],
        compiler_params=pltpu.CompilerParams(
            collective_id=0, has_side_effects=True, vmem_limit_bytes=16 << 20
        ),
    )(*(pltpu.with_memory_space_constraint(operand, pltpu.HBM) for operand in operands))
    return ladder / (occupied_shift[:, None] + virtual_shift[None, :])


def solution(mesh):
    torus = Mesh(
        mesh.devices.reshape(PLANES, 2, 2, mesh.shape["inner"]), (*TILE_AXES, "inner")
    )
    placed = (
        P(TILE_AXES, "inner"),
        P(TILE_AXES, "inner"),
        P(None, TILE_AXES),
        P(),
        P("inner"),
        P(TILE_AXES),
    )
    return jax.shard_map(
        on_device, mesh=torus, in_specs=placed, out_specs=P("inner", TILE_AXES), check_vma=False
    )
```

```python
import jax
import jax.numpy as jnp
from jax import lax
from jax.experimental import pallas as pl
from jax.experimental.pallas import tpu as pltpu
from jax.sharding import Mesh
from jax.sharding import PartitionSpec as P

TILE = 512
TILE_AXES = ("z", "y", "core")
MESH_ID = pl.DeviceIdType.MESH
PLANES = 16
PAIRS = 8
INNER = 8
QUADS = 4
LEFT = 4
RIGHT = 128
ROWS = 8
DEPTH = 16
LANES = 128
GROUP = PLANES * QUADS
CHUNKS = 4
PER = GROUP // CHUNKS


def kernel(
    a_ref, l_ref, r_ref, pattern_ref, out_ref,
    a_all, l_all, r_all, pattern, kron, m_out, m_in, s_out, s_in,
    gather_send, gather_recv, near_send, near_recv, m_send, m_recv, s_send, s_recv, own_sem, ready,
):
    z = lax.axis_index("z")
    y = lax.axis_index("y")
    core = lax.axis_index("core")
    inner = lax.axis_index("inner")
    quad = y * 2 + core
    place = z * QUADS + quad
    pair = z // 2
    parity = z % 2

    def plane_device(plane):
        return dict(z=plane, y=y, core=core, inner=inner)

    def near_device(step):
        return dict(
            z=z,
            y=y if step == 1 else 1 - y,
            core=core if step == 2 else 1 - core,
            inner=inner,
        )

    def near_quad(step):
        return (y if step == 1 else 1 - y) * 2 + (core if step == 2 else 1 - core)

    def inner_device(other):
        return dict(z=z, y=y, core=core, inner=other)

    def tile_device(spot):
        return dict(z=spot >> 2, y=(spot >> 1) & 1, core=spot & 1, inner=inner)

    def greet(semaphore, device):
        pl.semaphore_signal(semaphore, 1, device_id=device, device_id_type=MESH_ID)

    barrier = pltpu.get_barrier_semaphore()
    for step in range(1, INNER):
        greet(barrier, inner_device((inner + step) % INNER))
    for step in (4, 12, 2, 14):
        greet(barrier, plane_device((z + step) % PLANES))
    greet(barrier, plane_device(pair * 2 + 1 - parity))
    for step in (1, 2, 3):
        greet(barrier, near_device(step))

    own_a = pltpu.make_async_copy(a_ref, a_all.at[pair], own_sem.at[0])
    own_l = pltpu.make_async_copy(l_ref, l_all.at[parity, quad], own_sem.at[1])
    own_r = pltpu.make_async_copy(r_ref, r_all, own_sem.at[2])
    own_p = pltpu.make_async_copy(pattern_ref, pattern, own_sem.at[3])
    own_a.start()
    own_l.start()
    own_p.start()
    own_r.start()
    own_p.wait()
    mask = jnp.where(pattern[...] != 0, 1.0, 0.0).astype(jnp.bfloat16)
    spread = jnp.where(
        lax.broadcasted_iota(jnp.int32, (32, 256), 0)
        == lax.broadcasted_iota(jnp.int32, (32, 256), 1) >> 3,
        1.0,
        0.0,
    ).astype(jnp.bfloat16)
    spread = lax.dot_general(
        mask, spread, (((0,), (0,)), ((), ())), preferred_element_type=jnp.float32
    ).astype(jnp.bfloat16)
    same = jnp.where(
        (lax.broadcasted_iota(jnp.int32, (LANES, 256), 0) & 7)
        == (lax.broadcasted_iota(jnp.int32, (LANES, 256), 1) & 7),
        1.0,
        0.0,
    )
    lifted = lax.broadcasted_iota(jnp.int32, (LANES, RIGHT), 1) - (
        lax.broadcasted_iota(jnp.int32, (LANES, RIGHT), 0) >> 3
    )

    @pl.loop(0, RIGHT // 16)
    def _(block):
        lift = jnp.where(lifted == block * 16, 1.0, 0.0).astype(jnp.bfloat16)
        rows = jnp.dot(lift, spread, preferred_element_type=jnp.float32)
        kron[pl.ds(pl.multiple_of(block * LANES, LANES), LANES), :] = (rows * same).astype(
            jnp.bfloat16
        )

    pl.semaphore_wait(barrier, 5 + QUADS - 1 + INNER - 1)

    def factor_copy(src, side, step):
        spot = side * 4 + step
        mine = parity if side == 0 else 1 - parity
        return pltpu.make_async_remote_copy(
            src_ref=src,
            dst_ref=l_all.at[mine, quad],
            send_sem=near_send.at[spot],
            recv_sem=near_recv.at[spot],
            device_id=near_device(step) if step else plane_device(pair * 2 + 1 - parity),
            device_id_type=MESH_ID,
        )

    def factor_arrival(side, step):
        spot = side * 4 + step
        mine = parity if side == 0 else 1 - parity
        if step == 0:
            dst = l_all.at[1 - parity, quad]
        else:
            dst = l_all.at[mine, near_quad(step)]
        return pltpu.make_async_remote_copy(
            src_ref=l_ref,
            dst_ref=dst,
            send_sem=near_send.at[spot],
            recv_sem=near_recv.at[spot],
            device_id=plane_device(z),
            device_id_type=MESH_ID,
        )

    def gather_copy(slot, source, step, columns=slice(None), half=0):
        return pltpu.make_async_remote_copy(
            src_ref=(a_ref if source is pair else a_all.at[source]).at[:, columns],
            dst_ref=a_all.at[source, :, columns],
            send_sem=gather_send.at[slot],
            recv_sem=gather_recv.at[source, half],
            device_id=plane_device((pair + step) % PAIRS * 2 + parity),
            device_id_type=MESH_ID,
        )

    def gather_arrival(source, columns=slice(None), half=0):
        return pltpu.make_async_remote_copy(
            src_ref=a_ref.at[:, columns],
            dst_ref=a_all.at[source, :, columns],
            send_sem=gather_send.at[0],
            recv_sem=gather_recv.at[source, half],
            device_id=plane_device(z),
            device_id_type=MESH_ID,
        )

    width = a_ref.shape[1] // 2
    halves = [pl.ds(half * width, width) for half in range(2)]

    shared = [factor_copy(l_ref, 0, step) for step in range(4)]
    first = [
        gather_copy(side * 2 + half, pair, step, halves[half], half)
        for half in range(2)
        for side, step in enumerate((2, 6))
    ]
    second = [gather_copy(4 + side, pair, step) for side, step in enumerate((1, 7))]
    for copy in first + shared + second:
        copy.start()
    gathered = first + second
    factor_arrival(0, 0).wait_recv()
    passed = [factor_copy(l_all.at[1 - parity, quad], 1, step) for step in (1, 2, 3)]
    for copy in passed:
        copy.start()
    for half in range(2):
        for side, (back, on, over) in enumerate(((6, 1, 2), (2, 7, 6))):
            source = (pair + back) % PAIRS
            gather_arrival(source, halves[half], half).wait_recv()
            onward = [gather_copy(6 + side * 2 + half, source, on, halves[half], half)]
            for copy in onward:
                copy.start()
            gathered.extend(onward)
    for side, (back, over) in enumerate(((5, 1), (3, 7))):
        source = (pair + back) % PAIRS
        gather_arrival(source, halves[side], side).wait_recv()
        onward = gather_copy(10 + side, source, over, halves[side], side)
        onward.start()
        gathered.append(onward)

    own_a.wait()
    own_l.wait()
    for side in range(2):
        for step in (1, 2, 3):
            factor_arrival(side, step).wait_recv()

    def mix_copy(other):
        return pltpu.make_async_remote_copy(
            src_ref=m_out.at[other],
            dst_ref=m_in.at[inner],
            send_sem=m_send.at[other],
            recv_sem=m_recv.at[inner],
            device_id=inner_device(other),
            device_id_type=MESH_ID,
        )

    def mix_arrival(other):
        return pltpu.make_async_remote_copy(
            src_ref=m_out.at[other],
            dst_ref=m_in.at[other],
            send_sem=m_send.at[other],
            recv_sem=m_recv.at[other],
            device_id=inner_device(other),
            device_id_type=MESH_ID,
        )

    def tile_copy(spot):
        return pltpu.make_async_remote_copy(
            src_ref=s_out.at[spot],
            dst_ref=s_in.at[place],
            send_sem=s_send.at[spot],
            recv_sem=s_recv.at[place],
            device_id=tile_device(spot),
            device_id_type=MESH_ID,
        )

    def tile_arrival(spot):
        return pltpu.make_async_remote_copy(
            src_ref=s_out.at[spot],
            dst_ref=s_in.at[spot],
            send_sem=s_send.at[spot],
            recv_sem=s_recv.at[spot],
            device_id=tile_device(spot),
            device_id_type=MESH_ID,
        )

    for step in (0, 2, 6, 1, 7, 3, 5, 4):
        other = (pair + step) % PAIRS
        if step in (3, 4, 5):
            for half in ((0, 1) if step == 4 else (0,) if step == 3 else (1,)):
                gather_arrival(other, halves[half], half).wait_recv()
        elif step in (1, 7):
            gather_arrival(other).wait_recv()
        for left in range(LEFT):
            columns = pl.ds(left * TILE, TILE)
            m_out[other, left] = lax.dot_general(
                a_all[other, :, columns],
                l_all[:, :, :, columns].reshape(LANES, TILE),
                (((1,), (1,)), ((), ())),
                preferred_element_type=jnp.float32,
            )

        @pl.when(other != inner)
        def _(other=other):
            mix_copy(other).start()

    for step in (1, 2, 3):
        greet(ready, near_device(step))
    m_in[inner] = m_out[inner]
    pl.semaphore_wait(ready, QUADS - 1)

    @pl.loop(1, INNER)
    def _(step):
        mix_arrival((inner + step) % INNER).wait_recv()

    stacked = m_in[...].reshape(INNER * LEFT * ROWS, LANES)
    high = stacked.astype(jnp.bfloat16)
    low = (stacked - high.astype(jnp.float32)).astype(jnp.bfloat16)
    split = jnp.concatenate([high, low], axis=1)
    for chunk in range(CHUNKS):
        rows = pl.ds(chunk * PER * 2 * ROWS, PER * 2 * ROWS)
        both = jnp.dot(kron[rows, :], split, preferred_element_type=jnp.float32)
        both = both[:, :LANES] + both[:, LANES:]
        s_out[pl.ds(chunk * PER, PER)] = both.astype(jnp.bfloat16).reshape(PER, 2 * ROWS, LANES)

    @pl.loop(0, PLANES)
    def _(count):
        plane = (count & 8) + ((z + count) & 7)

        @pl.when(plane != z)
        def _():
            for turned in range(QUADS):
                tile_copy(plane * QUADS + (quad ^ turned)).start()

        @pl.when(plane == z)
        def _():
            for turned in range(1, QUADS):
                tile_copy(plane * QUADS + (quad ^ turned)).start()

    s_in[place] = s_out[place]

    own_r.wait()

    span = GROUP // 2
    for part in range(2):

        @pl.loop(part * span, part * span + span)
        def _(spot):
            @pl.when(spot != place)
            def _():
                tile_arrival(spot).wait_recv()

        mixed = jnp.concatenate(
            [s_in[pl.ds(part * span + eight * 8, 8)].reshape(LANES, LANES) for eight in range(span // 8)],
            axis=1,
        )
        depths = pl.ds(part * TILE, TILE)
        for side in range(2):
            columns = pl.ds(side * TILE, TILE)
            ladder = jnp.dot(mixed, r_all[depths, columns], preferred_element_type=jnp.float32)
            ladder = ladder.reshape(8, 2, ROWS, TILE)[:, side].reshape(8 * ROWS, TILE)
            out_ref[:, columns] = ladder if part == 0 else out_ref[:, columns] + ladder

    for copy in shared + passed + gathered:
        copy.wait_send()

    @pl.loop(1, INNER)
    def _(step):
        mix_arrival((inner + step) % INNER).wait_send()

    @pl.loop(1, GROUP)
    def _(step):
        tile_arrival((place + step) & (GROUP - 1)).wait_send()


def on_device(amplitudes, left_factors, right_factors, tile_pattern, occupied_shift, virtual_shift):
    width = amplitudes.shape[1]
    out_width = right_factors.shape[1]
    operands = (amplitudes, left_factors, right_factors, tile_pattern)
    ladder = pl.pallas_call(
        kernel,
        name="ladder",
        out_shape=jax.ShapeDtypeStruct((occupied_shift.shape[0], out_width), jnp.float32),
        in_specs=[pl.BlockSpec(memory_space=pltpu.HBM)] * 4,
        out_specs=pl.BlockSpec(memory_space=pltpu.VMEM),
        scratch_shapes=[
            pltpu.VMEM((PAIRS, ROWS, width), jnp.bfloat16),
            pltpu.VMEM((2, QUADS, DEPTH, width), jnp.bfloat16),
            pltpu.VMEM(right_factors.shape, jnp.bfloat16),
            pltpu.VMEM(tile_pattern.shape, jnp.int32),
            pltpu.VMEM((RIGHT * ROWS, 2 * LANES), jnp.bfloat16),
            pltpu.VMEM((INNER, LEFT, ROWS, LANES), jnp.float32),
            pltpu.VMEM((INNER, LEFT, ROWS, LANES), jnp.float32),
            pltpu.VMEM((GROUP, 2 * ROWS, LANES), jnp.bfloat16),
            pltpu.VMEM((GROUP, 2 * ROWS, LANES), jnp.bfloat16),
            pltpu.SemaphoreType.DMA((12,)),
            pltpu.SemaphoreType.DMA((PAIRS, 2)),
            pltpu.SemaphoreType.DMA((8,)),
            pltpu.SemaphoreType.DMA((8,)),
            pltpu.SemaphoreType.DMA((INNER,)),
            pltpu.SemaphoreType.DMA((INNER,)),
            pltpu.SemaphoreType.DMA((GROUP,)),
            pltpu.SemaphoreType.DMA((GROUP,)),
            pltpu.SemaphoreType.DMA((4,)),
            pltpu.SemaphoreType.REGULAR,
        ],
        compiler_params=pltpu.CompilerParams(
            collective_id=0, has_side_effects=True, vmem_limit_bytes=16 << 20
        ),
    )(*(pltpu.with_memory_space_constraint(operand, pltpu.HBM) for operand in operands))
    return ladder / (occupied_shift[:, None] + virtual_shift[None, :])


def solution(mesh):
    torus = Mesh(
        mesh.devices.reshape(PLANES, 2, 2, mesh.shape["inner"]), (*TILE_AXES, "inner")
    )
    placed = (
        P(TILE_AXES, "inner"),
        P(TILE_AXES, "inner"),
        P(None, TILE_AXES),
        P(),
        P("inner"),
        P(TILE_AXES),
    )
    return jax.shard_map(
        on_device, mesh=torus, in_specs=placed, out_specs=P("inner", TILE_AXES), check_vma=False
    )
```
